32 devices in a mesh: lat: 4 (over z), lon: 8 (over y, x, core).
Axes of the slice: x: 2, y: 2, z: 4, core: 2. Of those that a mesh axis runs over, the one named last changes fastest.
Arguments:
- state: bfloat16 [192, 64, 1024], P(None, 'lat', 'lon'), may hold values from -6 to 6
- depth_kernel: bfloat16 [192, 7, 7], replicated, may hold values from -0.875 to 0.875
- point_weight: bfloat16 [192, 192], replicated, may hold values from -0.4375 to 0.4375
- column_index: int32 [16384, 4], P(('lat', 'lon')), may hold values from 0 to 2047, as said below
- column_weight: bfloat16 [16384, 4], P(('lat', 'lon')), may hold values from 0.049804688 to 0.59765625
- owner: int32 [16384, 1], P(('lat', 'lon')), may hold values from 0 to 7; in each aligned block of 512 rows (0 to 511, 512 to 1023, ...) at most 64 rows name the same one
- observed: bfloat16 [16384, 137], P(('lat', 'lon')), may hold values from -6 to 6
- hidden_weight: bfloat16 [8, 192, 512], P('lon'), may hold values from -0.4375 to 0.4375
- level_weight: bfloat16 [8, 512, 137], P('lon'), may hold values from -0.25 to 0.25
- inverse_error: bfloat16 [8, 137], P('lon'), may hold values from 0.25 to 4
Outputs:
- gradient: bfloat16 [192, 64, 1024], P(None, 'lat', 'lon')
- departures: bfloat16 [16384, 137], P(('lat', 'lon'))
The draws below stay inside these ranges and needn't reach their ends.
Inputs may be any that keep to these rules, and one draw needn't show every extreme that they name: `column_index`: the four columns of one grid box of the sounding's own tile: b, b + 1, b + 128, b + 129. `owner`: among the 512 soundings of one tile no instrument appears more than 64 times.
All inputs are finite; a program needn't handle non-finite values.
Results may differ from the reference program's by a relative error of at most 0.0085.
Values may be sent and summed in bfloat16 or wider, within the bound.
A program may use at most 128 MiB of HBM per device.

```python
import math
import jax
import jax.numpy as jnp
import numpy as np
from jax import lax

C = 192
HID = 512
LEV = 137
TLAT = 16
TLON = 128
OBS_DEV = 512
CAP = 64
NLAT = 64
NLON = 1024
NSOUND = 16384
N_LAT = 4
N_LON = 8


def draw_column_index(key, part):
    base_lat = jax.random.randint(jax.random.fold_in(key, 11), (NSOUND, 1), 0, TLAT - 1)
    base_lon = jax.random.randint(jax.random.fold_in(key, 23), (NSOUND, 1), 0, TLON - 1)
    corner = base_lat * TLON + base_lon
    offsets = jnp.array([0, 1, TLON, TLON + 1], dtype=jnp.int32)
    return (corner + offsets[None, :]).astype(jnp.int32)


def block_levels(rng, extent, pieces, low, high):
    gain = 1.0
    for position, shards_of in pieces:
        draws = jax.random.uniform(jax.random.fold_in(jax.random.fold_in(rng, 6), position), (shards_of,), jnp.float32, low / len(pieces), high / len(pieces))
        gain = gain * jnp.repeat(jnp.exp(draws), extent[position] // shards_of).reshape((-1,) + (1,) * (len(extent) - 1 - position))
    return gain


def routed_block(key, own, number, rows, amount, top, bound, slope):
    ranking = jax.random.permutation(key, amount)
    packed, common = load_shares(amount, rows * top, bound, slope, True), load_shares(amount, rows * top, bound, slope, False)
    places = jnp.arange(amount)

    def named(sizes, turn):
        used = int((sizes > 0).sum())
        fixed = max(1, used // 4)
        passed = fixed + (places - fixed + turn * (used - fixed)) % max(1, amount - fixed)
        return jnp.zeros((amount,), jnp.int32).at[ranking[jnp.where(places < fixed, places, passed)]].set(jnp.asarray(sizes, jnp.int32))

    sizes = jnp.where(number % 4 == 0, named(packed, number // 4), named(common, number - number // 4 - 1))
    mixed = jax.random.permutation(jax.random.fold_in(own, 3), amount)
    donor, taker = mixed[0:amount // 2 * 2:2], mixed[1:amount // 2 * 2:2]
    margin = jnp.minimum(sizes[donor] - 1, bound - sizes[taker]) // 2
    margin = jnp.where((donor == ranking[0]) | (taker == ranking[0]) | (sizes[taker] == 0), 0, jnp.maximum(margin, 0))
    passed = jax.random.randint(jax.random.fold_in(own, 4), (amount // 2,), 0, 1 << 20) % (margin + 1)
    sizes = sizes.at[donor].add(-passed).at[taker].add(passed)
    labels = jnp.searchsorted(jnp.cumsum(sizes), jnp.arange(rows * top), side="right").astype(jnp.int32)
    listing = labels.reshape(top, rows).T
    listing = listing[jax.random.permutation(jax.random.fold_in(own, 1), rows)]
    turn = jax.random.randint(jax.random.fold_in(own, 2), (rows, 1), 0, top)
    return jnp.take_along_axis(listing, (jnp.arange(top)[None, :] + turn) % top, axis=1)


def load_shares(number_of, total, reach, skew, full):
    portions = [(1 << 20) // math.isqrt(rank ** skew) + 1 for rank in range(1, number_of + 1)]
    largest = reach if full else min(reach, max(-(-total // number_of), total * portions[0] // sum(portions)))
    least = 1 if total - largest >= number_of - 1 else 0
    counts, rest = [largest] + [least] * (number_of - 1), total - largest - least * (number_of - 1)
    while rest > 0:
        free = [i for i in range(1, number_of) if counts[i] < largest] or [i for i in range(1, number_of) if counts[i] < reach]
        pool, remaining = sum([portions[i] for i in free]), rest
        for i in free:
            extra = min(reach - counts[i], max(1, remaining * portions[i] // pool), rest)
            counts[i] = counts[i] + extra
            rest = rest - extra
    return np.array(counts)


def gaussian(key, extent, width, most, shards=(), held_as=jnp.bfloat16):
    level = block_levels(key, extent, shards, -0.22, 0.18) if shards else 1.0
    values = jax.random.normal(key, extent, jnp.float32) * width * level
    return jnp.minimum(jnp.maximum(values, -most), most).astype(held_as)


def setup_inputs(seed: int = 0) -> dict:
    keys = jax.random.split(jax.random.key(seed), 11)
    state = gaussian(keys[0], (C, NLAT, NLON), 1.0, 6.0, ((1, 4), (2, 8)))
    depth_kernel = gaussian(keys[1], (C, 7, 7), 49 ** -0.5, 0.875)
    point_weight = gaussian(keys[2], (C, C), C ** -0.5, 0.4375)
    column_index = draw_column_index(jax.random.fold_in(keys[10], 71), 0)
    column_weight = jnp.clip(0.049804688 + 0.54785156 * jax.random.uniform(keys[4], (NSOUND, 4), jnp.float32) ** block_levels(keys[4], (NSOUND, 4), ((0, 32),), -0.2, 0.2), 0.049804688, 0.59765625).astype(jnp.bfloat16)
    owner_keys = jax.random.split(jax.random.fold_in(keys[5], 1), NSOUND // OBS_DEV)
    owner_turns = jax.random.permutation(jax.random.fold_in(keys[5], 3), NSOUND // OBS_DEV)
    owner = jax.vmap(lambda own, number: routed_block(jax.random.fold_in(keys[5], 2), own, number, OBS_DEV, N_LON, 1, CAP, 2))(owner_keys, owner_turns).reshape((NSOUND, 1))
    observed = gaussian(keys[6], (NSOUND, LEV), 1.0, 6.0, ((0, 32),))
    hidden_weight = gaussian(keys[7], (N_LON, C, HID), C ** -0.5, 0.4375, ((0, 8),))
    level_weight = gaussian(keys[8], (N_LON, HID, LEV), HID ** -0.5, 0.25, ((0, 8),))
    inverse_error = jnp.clip(jnp.exp(math.log(4.0) - 2.7725887 * jax.random.uniform(keys[9], (N_LON, LEV), jnp.float32) ** block_levels(keys[9], (N_LON, LEV), ((0, 8),), -0.2, 0.2)), 0.25, 4.0).astype(jnp.bfloat16)
    return dict(state=state, depth_kernel=depth_kernel, point_weight=point_weight, column_index=column_index, column_weight=column_weight, owner=owner, observed=observed, hidden_weight=hidden_weight, level_weight=level_weight, inverse_error=inverse_error)


def rounded(values):
    return lax.optimization_barrier(values.astype(jnp.bfloat16))

def pad_grid(values):
    values = jnp.pad(values, ((0, 0), (3, 3), (0, 0)))
    return jnp.pad(values, ((0, 0), (0, 0), (3, 3)), mode='wrap')

def depthwise(values, kernel):
    height = values.shape[1]
    breadth = values.shape[2]
    padded = pad_grid(values)

    def one_channel(pair):
        plane, weights_c = pair
        weights_c = weights_c.astype(jnp.float32)
        summed = jnp.zeros((height, breadth), jnp.float32)
        for row_tap in range(7):
            for col_tap in range(7):
                summed = summed + weights_c[row_tap, col_tap] * plane[row_tap:row_tap + height, col_tap:col_tap + breadth].astype(jnp.float32)
        return summed
    return lax.map(one_channel, (padded, kernel))

def observe(profiles, observed, hidden_w, level_w, inverse_e):
    pre_act = jnp.dot(profiles, hidden_w, preferred_element_type=jnp.float32)
    squashed = jnp.tanh(pre_act)
    levels = jnp.dot(rounded(squashed), level_w, preferred_element_type=jnp.float32)
    misfit = levels - observed.astype(jnp.float32)
    weighted = rounded(inverse_e.astype(jnp.float32)[None, :] * misfit)
    back_hidden = jnp.dot(weighted, level_w.T, preferred_element_type=jnp.float32)
    back_pre = rounded(back_hidden * (1.0 - squashed * squashed))
    adjoint = jnp.dot(back_pre, hidden_w.T, preferred_element_type=jnp.float32)
    return (adjoint.astype(jnp.bfloat16), misfit.astype(jnp.bfloat16))

def reference(state, depth_kernel, point_weight, column_index, column_weight, owner, observed, hidden_weight, level_weight, inverse_error):
    devices_n = N_LAT * N_LON
    cells = NLAT * NLON
    mixed = rounded(depthwise(state, depth_kernel)).reshape(C, cells)
    pre_gelu = jnp.dot(point_weight.T, mixed, preferred_element_type=jnp.float32)
    analysis = rounded(state.reshape(C, cells).astype(jnp.float32) + jax.nn.gelu(pre_gelu))
    device = jnp.arange(NSOUND, dtype=jnp.int32) // OBS_DEV
    tile_lat = device // N_LON
    tile_lon = device % N_LON
    local_lat = column_index // TLON
    local_lon = column_index % TLON
    global_index = ((tile_lat[:, None] * TLAT + local_lat) * NLON + tile_lon[:, None] * TLON + local_lon).astype(jnp.int32)
    weights_f = column_weight.astype(jnp.float32)
    profile_t = jnp.zeros((C, NSOUND), jnp.float32)
    for corner in range(4):
        profile_t = profile_t + analysis[:, global_index[:, corner]].astype(jnp.float32) * weights_f[:, corner][None, :]
    profiles = profile_t.T.astype(jnp.bfloat16)
    sounding = owner[:, 0].reshape(devices_n, OBS_DEV)
    onehot = (sounding[:, :, None] == jnp.arange(N_LON, dtype=jnp.int32)[None, None, :]).astype(jnp.int32)
    before = jnp.cumsum(onehot, axis=1) - onehot
    within = lax.optimization_barrier(jnp.sum(before * onehot, axis=2))
    slot_of = (sounding * CAP + within).astype(jnp.int32)
    device_ids = jnp.broadcast_to(jnp.arange(devices_n, dtype=jnp.int32)[:, None], (devices_n, OBS_DEV))
    buffer_prof = jnp.zeros((devices_n, N_LON * CAP, C), jnp.bfloat16).at[device_ids, slot_of].set(profiles.reshape(devices_n, OBS_DEV, C))
    buffer_obs = jnp.zeros((devices_n, N_LON * CAP, LEV), jnp.bfloat16).at[device_ids, slot_of].set(observed.reshape(devices_n, OBS_DEV, LEV))
    by_instrument_prof = buffer_prof.reshape(devices_n, N_LON, CAP, C).transpose(1, 0, 2, 3).reshape(N_LON, devices_n * CAP, C)
    by_instrument_obs = buffer_obs.reshape(devices_n, N_LON, CAP, LEV).transpose(1, 0, 2, 3).reshape(N_LON, devices_n * CAP, LEV)

    def per_instrument(group):
        return observe(group[0], group[1], group[2], group[3], group[4])
    adjoint_all, misfit_all = lax.map(per_instrument, (by_instrument_prof, by_instrument_obs, hidden_weight, level_weight, inverse_error))
    adjoint_all = adjoint_all.reshape(N_LON, devices_n, CAP, C).transpose(1, 0, 2, 3).reshape(devices_n, N_LON * CAP, C)
    misfit_all = misfit_all.reshape(N_LON, devices_n, CAP, LEV).transpose(1, 0, 2, 3).reshape(devices_n, N_LON * CAP, LEV)
    adjoint_profiles = adjoint_all[device_ids, slot_of].reshape(NSOUND, C)
    departures = misfit_all[device_ids, slot_of].reshape(NSOUND, LEV)
    adjoint_f = adjoint_profiles.astype(jnp.float32)
    feedback = jnp.zeros((C, cells), jnp.float32)
    for corner in range(4):
        feedback = feedback.at[:, global_index[:, corner]].add((adjoint_f * weights_f[:, corner][:, None]).T)
    unused, pull_back = jax.vjp(jax.nn.gelu, pre_gelu)
    gate_back = pull_back(feedback)[0].astype(jnp.bfloat16)
    mixed_back = rounded(jnp.dot(point_weight, gate_back, preferred_element_type=jnp.float32)).reshape(C, NLAT, NLON)
    spread_back = depthwise(mixed_back, depth_kernel[:, ::-1, ::-1])
    gradient = (feedback.reshape(C, NLAT, NLON) + spread_back).astype(jnp.bfloat16)
    return (gradient, departures)
```

```python
import jax
import jax.numpy as jnp
from jax import lax
from jax.experimental import pallas as pl
from jax.experimental.pallas import tpu as pltpu
from jax.sharding import PartitionSpec as P

CAP = 64
F32 = jnp.float32
BF = jnp.bfloat16
VM = pl.BlockSpec(memory_space=pltpu.VMEM)


def nn(a, b):
    return jnp.dot(a, b, preferred_element_type=F32)


def nt(a, b):
    return lax.dot_general(a, b, (((1,), (1,)), ((), ())), preferred_element_type=F32)


def call(kernel, out_shape, scratch, flops, nbytes, *args):
    return pl.pallas_call(
        kernel,
        out_shape=out_shape,
        in_specs=[VM] * len(args),
        out_specs=jax.tree.map(lambda _: VM, out_shape),
        scratch_shapes=scratch,
        cost_estimate=pl.CostEstimate(flops=flops, bytes_accessed=nbytes, transcendentals=0),
        compiler_params=pltpu.CompilerParams(vmem_limit_bytes=56 << 20),
    )(*args)


def conv_group(x_ref, h_ref, k_ref, base, flip):
    rows = x_ref.shape[0]
    breadth = x_ref.shape[2]
    height = rows - 6
    lane = lax.broadcasted_iota(jnp.int32, (16, breadth), 1)
    taps = k_ref[pl.ds(base, 16), :]
    acc = [None] * height
    for col in range(7):
        shift = col - 3
        weights = []
        for row in range(7):
            t = (6 - row) * 7 + 6 - col if flip else row * 7 + col
            weights.append(jnp.broadcast_to(taps[:, t : t + 1], (16, breadth)))
        for r in range(rows):
            v = x_ref[r, pl.ds(base, 16), :].astype(F32)
            if shift:
                edge = h_ref[r, pl.ds(base, 16), :].astype(F32)
                mask = lane < shift if shift > 0 else lane >= breadth + shift
                v = pltpu.roll(jnp.where(mask, edge, v), (-shift) % breadth, 1)
            for row in range(7):
                i = r - row
                if 0 <= i < height:
                    term = weights[row] * v
                    acc[i] = term if acc[i] is None else acc[i] + term
    return acc


def prep_kernel(owner_row, owner_col, row0, col0, w_ref, obs_ref, wt_ref, p_ref, pt_ref, obs_slot):
    height, obs, breadth = wt_ref.shape
    slots = p_ref.shape[0]
    n = slots // CAP
    lane = lax.broadcasted_iota(jnp.int32, (obs, breadth), 1)
    c0 = jnp.broadcast_to(col0[...], (obs, breadth))
    r0 = jnp.broadcast_to(row0[...], (obs, breadth))
    w = w_ref[...].astype(F32)
    zero = jnp.zeros((obs, breadth), F32)
    first = lane == c0
    second = lane == c0 + 1
    top = jnp.where(first, w[:, 0:1], jnp.where(second, w[:, 1:2], zero))
    bottom = jnp.where(first, w[:, 2:3], jnp.where(second, w[:, 3:4], zero))
    for r in range(height):
        wt_ref[r] = jnp.where(r0 == r, top, jnp.where(r0 == r - 1, bottom, zero)).astype(BF)
    si = lax.broadcasted_iota(jnp.int32, (obs, obs), 0)
    sj = lax.broadcasted_iota(jnp.int32, (obs, obs), 1)
    ones_u = jnp.where(si < sj, 1.0, 0.0).astype(BF)
    ones_l = jnp.where(sj < si, 1.0, 0.0).astype(BF)
    own = owner_row[...]
    hot = jnp.where(lax.broadcasted_iota(jnp.int32, (n, obs), 0) == own, 1.0, 0.0)
    within = jnp.sum(nn(hot.astype(BF), ones_u) * hot, axis=0, keepdims=True)
    slot_row = own * CAP + within.astype(jnp.int32)
    place = lax.broadcasted_iota(jnp.int32, (slots, obs), 0) == slot_row
    p = jnp.where(place, 1.0, 0.0).astype(BF)
    p_ref[...] = p
    own = owner_col[...]
    hot = jnp.where(lax.broadcasted_iota(jnp.int32, (obs, 128), 1) == own, 1.0, 0.0)
    within = jnp.sum(nn(ones_l, hot.astype(BF)) * hot, axis=1, keepdims=True)
    slot_col = own * CAP + within.astype(jnp.int32)
    place = lax.broadcasted_iota(jnp.int32, (obs, slots), 1) == slot_col
    pt_ref[...] = jnp.where(place, 1.0, 0.0).astype(BF)
    obs_slot[...] = nn(p, obs_ref[...]).astype(BF)


def forward_kernel(x_ref, h_ref, k_ref, pwt_ref, wt_ref, p_ref, dg_ref, prof_ref, mixed, total):
    rows, channels, breadth = x_ref.shape
    height = rows - 6

    def group(g, carry):
        base = pl.multiple_of(g * 16, 16)
        for i, v in enumerate(conv_group(x_ref, h_ref, k_ref, base, False)):
            mixed[i, pl.ds(base, 16), :] = v.astype(BF)
        return carry

    lax.fori_loop(0, channels // 16, group, 0)
    total[...] = jnp.zeros_like(total)
    a, b = 0.7978845608028654, 0.044715

    def pair(q, carry):
        r = q * 2
        pre = nn(pwt_ref[...], jnp.concatenate([mixed[r], mixed[r + 1]], axis=1))
        square = pre * pre
        t = jnp.tanh(a * (pre + b * (square * pre)))
        half = 0.5 * (1.0 + t)
        slope = half + (0.5 * pre) * (1.0 - t * t) * (a * (1.0 + (3.0 * b) * square))
        dg_ref[r] = slope[:, :breadth]
        dg_ref[r + 1] = slope[:, breadth:]
        state = jnp.concatenate([x_ref[r + 3], x_ref[r + 4]], axis=1).astype(F32)
        analysis = (state + pre * half).astype(BF)
        total[...] += nt(jnp.concatenate([wt_ref[r], wt_ref[r + 1]], axis=1), analysis)
        return carry

    lax.fori_loop(0, height // 2, pair, 0)
    prof_ref[...] = nn(p_ref[...], total[...].astype(BF)).astype(BF)


def middle_kernel(levels, prof_ref, obs_ref, op_ref, wt_ref, pt_ref, dg_ref, pw_ref, dep_ref, fb_ref, mb_ref, adj, mis):
    height, channels, breadth = dg_ref.shape
    n = op_ref.shape[0]
    err_row = op_ref.shape[1] - 16

    def instrument(o, carry):
        at = pl.ds(pl.multiple_of(o * CAP, CAP), CAP)
        hw = op_ref[o, :channels, :]
        lw = op_ref[o, channels : channels + levels, :]
        err = op_ref[o, err_row : err_row + 1, :levels].astype(F32)
        squashed = jnp.tanh(nn(prof_ref[at, :], hw))
        misfit = nt(squashed.astype(BF), lw) - obs_ref[at, :].astype(F32)
        mis[at, :] = misfit.astype(BF)
        back = nn((err * misfit).astype(BF), lw) * (1.0 - squashed * squashed)
        adj[at, :] = nt(back.astype(BF), hw).astype(BF)
        return carry

    lax.fori_loop(0, n, instrument, 0)
    dep_ref[...] = nn(pt_ref[...], mis[...]).astype(BF)
    adj_t = nn(pt_ref[...], adj[...]).T.astype(BF)

    def pair(q, carry):
        r = q * 2
        fb = nn(adj_t, jnp.concatenate([wt_ref[r], wt_ref[r + 1]], axis=1))
        fb_ref[r] = fb[:, :breadth]
        fb_ref[r + 1] = fb[:, breadth:]
        gate = (fb * jnp.concatenate([dg_ref[r], dg_ref[r + 1]], axis=1)).astype(BF)
        mb = nn(pw_ref[...], gate).astype(BF)
        mb_ref[r] = mb[:, :breadth]
        mb_ref[r + 1] = mb[:, breadth:]
        return carry

    lax.fori_loop(0, height // 2, pair, 0)


def backward_kernel(x_ref, h_ref, k_ref, fb_ref, out_ref):
    channels = x_ref.shape[1]

    def group(g, carry):
        base = pl.multiple_of(g * 16, 16)
        for i, v in enumerate(conv_group(x_ref, h_ref, k_ref, base, True)):
            out_ref[i, pl.ds(base, 16), :] = (v + fb_ref[i, pl.ds(base, 16), :]).astype(BF)
        return carry

    lax.fori_loop(0, channels // 16, group, 0)


def halo(x):
    lat, lon = lax.axis_size("lat"), lax.axis_size("lon")
    up = [(i, i + 1) for i in range(lat - 1)]
    down = [(i + 1, i) for i in range(lat - 1)]
    right = [(i, (i + 1) % lon) for i in range(lon)]
    left = [((i + 1) % lon, i) for i in range(lon)]
    x = jnp.concatenate(
        [lax.ppermute(x[-3:], "lat", up), x, lax.ppermute(x[:3], "lat", down)], axis=0
    )
    rows, channels, breadth = x.shape
    head = lax.ppermute(x[:, :, :3].transpose(2, 0, 1), "lon", left).transpose(1, 2, 0)
    tail = lax.ppermute(x[:, :, -3:].transpose(2, 0, 1), "lon", right).transpose(1, 2, 0)
    edge = jnp.concatenate([head, jnp.zeros((rows, channels, breadth - 6), x.dtype), tail], axis=2)
    return x, edge


def body(
    state,
    depth_kernel,
    point_weight,
    column_index,
    column_weight,
    owner,
    observed,
    hidden_weight,
    level_weight,
    inverse_error,
):
    channels, height, breadth = state.shape
    obs, levels = observed.shape
    hid = hidden_weight.shape[2]
    n = lax.axis_size("lon")
    slots = n * CAP
    sds = jax.ShapeDtypeStruct
    fill = (-(channels + levels)) % 16
    pack = jnp.concatenate(
        [
            hidden_weight[0],
            jnp.pad(level_weight[0].T, ((0, fill), (0, 0))),
            jnp.pad(inverse_error, ((0, 15), (0, hid - levels))),
        ],
        axis=0,
    )
    operators = lax.all_gather(pack[None], "lon", axis=0, tiled=True)
    taps = jnp.pad(depth_kernel.reshape(channels, 49).astype(F32), ((0, 0), (0, 79)))
    x, edge = halo(state.transpose(1, 0, 2))
    row0 = column_index[:, :1] // breadth
    col0 = column_index[:, :1] - row0 * breadth
    wt, p, pt, obs_slot = call(
        prep_kernel,
        (sds((height, obs, breadth), BF), sds((slots, obs), BF), sds((obs, slots), BF), sds((slots, levels), BF)),
        [],
        10**8,
        4 << 20,
        owner.reshape(1, obs),
        owner,
        row0,
        col0,
        column_weight,
        observed,
    )
    slope, prof = call(
        forward_kernel,
        (sds((height, channels, breadth), F32), sds((slots, channels), BF)),
        [pltpu.VMEM((height, channels, breadth), BF), pltpu.VMEM((obs, channels), F32)],
        10**9,
        8 << 20,
        x,
        edge,
        taps,
        point_weight.T,
        wt,
        p,
    )
    departures, fb, mb = call(
        lambda *refs: middle_kernel(levels, *refs),
        (sds((obs, levels), BF), sds((height, channels, breadth), F32), sds((height, channels, breadth), BF)),
        [pltpu.VMEM((slots, channels), BF), pltpu.VMEM((slots, levels), BF)],
        10**9,
        12 << 20,
        prof,
        obs_slot,
        operators,
        wt,
        pt,
        slope,
        point_weight,
    )
    x, edge = halo(mb)
    grad = call(
        backward_kernel,
        sds((height, channels, breadth), BF),
        [],
        10**9,
        8 << 20,
        x,
        edge,
        taps,
        fb,
    )
    return (grad.transpose(1, 0, 2), departures)


def solution(mesh):
    in_specs = (
        P(None, "lat", "lon"),
        P(),
        P(),
        P(("lat", "lon"), None),
        P(("lat", "lon"), None),
        P(("lat", "lon"), None),
        P(("lat", "lon"), None),
        P("lon", None, None),
        P("lon", None, None),
        P("lon", None),
    )
    out_specs = (P(None, "lat", "lon"), P(("lat", "lon"), None))
    return jax.shard_map(body, mesh=mesh, in_specs=in_specs, out_specs=out_specs, check_vma=False)
```

```python
import jax
import jax.numpy as jnp
from jax import lax
from jax.experimental import pallas as pl
from jax.experimental.pallas import tpu as pltpu
from jax.sharding import PartitionSpec as P

CAP = 64
F32 = jnp.float32
BF = jnp.bfloat16
VM = pl.BlockSpec(memory_space=pltpu.VMEM)


def nn(a, b):
    return jnp.dot(a, b, preferred_element_type=F32)


def nt(a, b):
    return lax.dot_general(a, b, (((1,), (1,)), ((), ())), preferred_element_type=F32)


def conv_group(x_ref, h_ref, k_ref, base, flip):
    rows = x_ref.shape[0]
    breadth = x_ref.shape[2]
    height = rows - 6
    lane = lax.broadcasted_iota(jnp.int32, (16, breadth), 1)
    taps = k_ref[pl.ds(base, 16), :]
    acc = [None] * height
    for col in range(7):
        shift = col - 3
        weights = []
        for row in range(7):
            t = (6 - row) * 7 + 6 - col if flip else row * 7 + col
            weights.append(jnp.broadcast_to(taps[:, t : t + 1], (16, breadth)))
        for r in range(rows):
            v = x_ref[r, pl.ds(base, 16), :].astype(F32)
            if shift:
                edge = h_ref[r, pl.ds(base, 16), :].astype(F32)
                mask = lane < shift if shift > 0 else lane >= breadth + shift
                v = pltpu.roll(jnp.where(mask, edge, v), (-shift) % breadth, 1)
            for row in range(7):
                i = r - row
                if 0 <= i < height:
                    term = weights[row] * v
                    acc[i] = term if acc[i] is None else acc[i] + term
    return acc


def prepare(owner_row, owner_col, row0, col0, w_ref, obs_ref, wt_ref, p_ref, pt_ref, obs_slot):
    height, obs, breadth = wt_ref.shape
    slots = p_ref.shape[0]
    n = slots // CAP
    lane = lax.broadcasted_iota(jnp.int32, (obs, breadth), 1)
    c0 = jnp.broadcast_to(col0[...], (obs, breadth))
    r0 = jnp.broadcast_to(row0[...], (obs, breadth))
    w = w_ref[...].astype(F32)
    zero = jnp.zeros((obs, breadth), F32)
    first = lane == c0
    second = lane == c0 + 1
    top = jnp.where(first, w[:, 0:1], jnp.where(second, w[:, 1:2], zero))
    bottom = jnp.where(first, w[:, 2:3], jnp.where(second, w[:, 3:4], zero))
    for r in range(height):
        wt_ref[r] = jnp.where(r0 == r, top, jnp.where(r0 == r - 1, bottom, zero)).astype(BF)
    si = lax.broadcasted_iota(jnp.int32, (obs, obs), 0)
    sj = lax.broadcasted_iota(jnp.int32, (obs, obs), 1)
    ones_u = jnp.where(si < sj, 1.0, 0.0).astype(BF)
    ones_l = jnp.where(sj < si, 1.0, 0.0).astype(BF)
    own = owner_row[...]
    hot = jnp.where(lax.broadcasted_iota(jnp.int32, (n, obs), 0) == own, 1.0, 0.0)
    within = jnp.sum(nn(hot.astype(BF), ones_u) * hot, axis=0, keepdims=True)
    slot_row = own * CAP + within.astype(jnp.int32)
    place = lax.broadcasted_iota(jnp.int32, (slots, obs), 0) == slot_row
    p = jnp.where(place, 1.0, 0.0).astype(BF)
    p_ref[...] = p
    own = owner_col[...]
    hot = jnp.where(lax.broadcasted_iota(jnp.int32, (obs, 128), 1) == own, 1.0, 0.0)
    within = jnp.sum(nn(ones_l, hot.astype(BF)) * hot, axis=1, keepdims=True)
    slot_col = own * CAP + within.astype(jnp.int32)
    place = lax.broadcasted_iota(jnp.int32, (obs, slots), 1) == slot_col
    pt_ref[...] = jnp.where(place, 1.0, 0.0).astype(BF)
    obs_slot[...] = nn(p, obs_ref[...]).astype(BF)


def remote(src, dst, send, recv, device):
    return pltpu.make_async_remote_copy(
        src_ref=src,
        dst_ref=dst,
        send_sem=send,
        recv_sem=recv,
        device_id=device,
        device_id_type=pl.DeviceIdType.MESH,
    )


def selector(breadth):
    s = lax.broadcasted_iota(jnp.int32, (8, breadth), 0)
    lane = lax.broadcasted_iota(jnp.int32, (8, breadth), 1)
    near = (s < 3) & (lane == s)
    far = (s > 4) & (lane == s + (breadth - 8))
    return jnp.where(near | far, 1.0, 0.0).astype(BF)


def copies(src, off, x, edge, right_in, left_in, send, recv, lats, lons):
    height = edge.shape[0]
    lat, lon = lax.axis_index("lat"), lax.axis_index("lon")
    left, right = lax.rem(lon + lons - 1, lons), lax.rem(lon + 1, lons)
    low, high, mid = pl.ds(0, 3), pl.ds(height + 3, 3), pl.ds(3, height)
    end = pl.ds(height - 3, 3)

    def make(i, a, b, device):
        return remote(a, b, send.at[i], recv.at[i], device)

    side = [
        make(2, edge, right_in.at[mid], {"lat": lat, "lon": left}),
        make(3, edge, left_in.at[mid], {"lat": lat, "lon": right}),
    ]
    u, d = lax.max(lat - 1, 0), lax.min(lat + 1, lats - 1)
    up = [
        make(0, src.at[pl.ds(off, 3)], x.at[high], {"lat": u, "lon": lon}),
        make(4, edge.at[low], right_in.at[high], {"lat": u, "lon": left}),
        make(5, edge.at[low], left_in.at[high], {"lat": u, "lon": right}),
    ]
    down = [
        make(1, src.at[pl.ds(off + height - 3, 3)], x.at[low], {"lat": d, "lon": lon}),
        make(6, edge.at[end], right_in.at[low], {"lat": d, "lon": left}),
        make(7, edge.at[end], left_in.at[low], {"lat": d, "lon": right}),
    ]
    return lat > 0, lat < lats - 1, up, down, side


def start_exchange(src, off, x, edge, right_in, left_in, send, recv, lats, lons):
    height = edge.shape[0]
    pick = selector(x.shape[2])
    has_up, has_down, up, down, side = copies(
        src, off, x, edge, right_in, left_in, send, recv, lats, lons
    )
    pl.when(has_up)(lambda: up[0].start())
    pl.when(has_down)(lambda: down[0].start())

    def row(r, carry):
        edge[r] = nt(pick, src[off + r]).astype(BF)
        return carry

    lax.fori_loop(0, height, row, 0, unroll=4)
    for copy in side:
        copy.start()

    @pl.when(has_up)
    def _():
        up[1].start()
        up[2].start()

    @pl.when(has_down)
    def _():
        down[1].start()
        down[2].start()

    for missing, at in ((lat_first(has_up), 0), (lat_first(has_down), height + 3)):

        @pl.when(missing)
        def _():
            for ref in (x, right_in, left_in):
                ref[at : at + 3] = jnp.zeros((3,) + ref.shape[1:], BF)


def lat_first(has):
    return jnp.logical_not(has)


def end_exchange(src, off, x, edge, right_in, left_in, halo, send, recv, lats, lons):
    has_up, has_down, up, down, side = copies(
        src, off, x, edge, right_in, left_in, send, recv, lats, lons
    )

    @pl.when(has_up)
    def _():
        for copy in down:
            copy.wait_recv()
        for copy in up:
            copy.wait_send()

    @pl.when(has_down)
    def _():
        for copy in up:
            copy.wait_recv()
        for copy in down:
            copy.wait_send()

    for copy in side:
        copy.wait()
    pick = selector(x.shape[2])
    near = lax.broadcasted_iota(jnp.int32, (8, x.shape[1]), 0) < 4

    def row(r, carry):
        both = jnp.where(near, right_in[r].astype(F32), left_in[r].astype(F32))
        halo[r] = nn(both.T.astype(BF), pick).astype(BF)
        return carry

    lax.fori_loop(0, x.shape[0], row, 0, unroll=2)


def kernel(
    lats,
    lons,
    state,
    op_ref,
    owner_row,
    owner_col,
    row0,
    col0,
    w_ref,
    obs_ref,
    k_ref,
    pwt_ref,
    pw_ref,
    out_ref,
    dep_ref,
    x1,
    x2,
    halo,
    edge,
    right_in,
    left_in,
    ops,
    wt,
    p_mat,
    pt_mat,
    obs_slot,
    mixed,
    grid_f,
    total,
    prof,
    adj,
    mis,
    send,
    recv,
    op_send,
    op_recv,
):
    height, channels, breadth = state.shape
    levels = obs_ref.shape[1]
    lat, lon = lax.axis_index("lat"), lax.axis_index("lon")
    partner = lon + 1 - 2 * lax.rem(lon, 2)
    other = lax.rem(lon + lons - 1 + 2 * lax.rem(lon, 2), lons)
    half = lons // 2
    peers = [lax.rem(lon + 2 * j, lons) for j in range(1, half)]
    barrier = pltpu.get_barrier_semaphore()

    def greet(a, b):
        pl.semaphore_signal(
            barrier,
            inc=1,
            device_id={"lat": a, "lon": b},
            device_id_type=pl.DeviceIdType.MESH,
        )

    for b in [partner, other] + peers:
        greet(lat, b)

    @pl.when(lat > 0)
    def _():
        for b in (partner, lon, other):
            greet(lat - 1, b)

    @pl.when(lat < lats - 1)
    def _():
        for b in (partner, lon, other):
            greet(lat + 1, b)

    sides = lax.min(lat, 1) + lax.min(lats - 1 - lat, 1)
    pl.semaphore_wait(barrier, half + 1 + 3 * sides)

    def wires(k):
        return edge.at[k], right_in.at[k], left_in.at[k]

    start_exchange(state, 0, x1, *wires(0), send.at[0], recv.at[0], lats, lons)
    sends = [
        remote(op_ref, ops.at[lon], op_send.at[j], op_recv.at[lon], {"lat": lat, "lon": b})
        for j, b in enumerate([partner] + peers)
    ]
    for copy in sends:
        copy.start()
    x1[3 : 3 + height] = state[...]
    ops[lon] = op_ref[...]
    prepare(owner_row, owner_col, row0, col0, w_ref, obs_ref, wt, p_mat, pt_mat, obs_slot)
    end_exchange(state, 0, x1, *wires(0), halo, send.at[0], recv.at[0], lats, lons)

    def group(g, carry):
        base = pl.multiple_of(g * 16, 16)
        for i, v in enumerate(conv_group(x1, halo, k_ref, base, False)):
            mixed[i, pl.ds(base, 16), :] = v.astype(BF)
        return carry

    lax.fori_loop(0, channels // 16, group, 0)

    forwards = []
    for j, b in enumerate(peers):
        copy = remote(
            ops.at[b], ops.at[b], op_send.at[half + j], op_recv.at[b], {"lat": lat, "lon": partner}
        )
        copy.wait_recv()
        copy.start()
        forwards.append(copy)

    total[...] = jnp.zeros_like(total)
    a, c3 = 0.7978845608028654, 0.044715

    def ahead(q, carry):
        r = q * 2
        pre = nn(pwt_ref[...], jnp.concatenate([mixed[r], mixed[r + 1]], axis=1))
        square = pre * pre
        t = jnp.tanh(a * (pre + c3 * (square * pre)))
        gate = 0.5 * (1.0 + t)
        slope = gate + (0.5 * pre) * (1.0 - t * t) * (a * (1.0 + (3.0 * c3) * square))
        grid_f[r] = slope[:, :breadth]
        grid_f[r + 1] = slope[:, breadth:]
        here = jnp.concatenate([state[r], state[r + 1]], axis=1).astype(F32)
        analysis = (here + pre * gate).astype(BF)
        total[...] += nt(jnp.concatenate([wt[r], wt[r + 1]], axis=1), analysis)
        return carry

    lax.fori_loop(0, height // 2, ahead, 0)
    prof[...] = nn(p_mat[...], total[...].astype(BF)).astype(BF)

    for j in range(half):
        b = lax.rem(partner + 2 * j, lons)
        remote(
            ops.at[b], ops.at[b], op_send.at[0], op_recv.at[b], {"lat": lat, "lon": partner}
        ).wait_recv()
    err_row = op_ref.shape[0] - 16

    def instrument(o, carry):
        at = pl.ds(pl.multiple_of(o * CAP, CAP), CAP)
        hw = ops[o, :channels, :]
        lw = ops[o, channels : channels + levels, :]
        err = ops[o, err_row : err_row + 1, :levels].astype(F32)
        squashed = jnp.tanh(nn(prof[at, :], hw))
        misfit = nt(squashed.astype(BF), lw) - obs_slot[at, :].astype(F32)
        mis[at, :] = misfit.astype(BF)
        back = nn((err * misfit).astype(BF), lw) * (1.0 - squashed * squashed)
        adj[at, :] = nt(back.astype(BF), hw).astype(BF)
        return carry

    lax.fori_loop(0, lons, instrument, 0, unroll=4)
    dep_ref[...] = nn(pt_mat[...], mis[...]).astype(BF)
    adj_t = nn(pt_mat[...], adj[...]).T.astype(BF)

    def behind(q, carry):
        r = q * 2
        fb = nn(adj_t, jnp.concatenate([wt[r], wt[r + 1]], axis=1))
        gate = (fb * jnp.concatenate([grid_f[r], grid_f[r + 1]], axis=1)).astype(BF)
        grid_f[r] = fb[:, :breadth]
        grid_f[r + 1] = fb[:, breadth:]
        mb = nn(pw_ref[...], gate).astype(BF)
        x2[r + 3] = mb[:, :breadth]
        x2[r + 4] = mb[:, breadth:]
        return carry

    lax.fori_loop(0, height // 2, behind, 0)
    for copy in sends + forwards:
        copy.wait_send()
    start_exchange(x2, 3, x2, *wires(1), send.at[1], recv.at[1], lats, lons)
    end_exchange(x2, 3, x2, *wires(1), halo, send.at[1], recv.at[1], lats, lons)

    def group_back(g, carry):
        base = pl.multiple_of(g * 16, 16)
        for i, v in enumerate(conv_group(x2, halo, k_ref, base, True)):
            out_ref[i, pl.ds(base, 16), :] = (v + grid_f[i, pl.ds(base, 16), :]).astype(BF)
        return carry

    lax.fori_loop(0, channels // 16, group_back, 0)


def body(
    state,
    depth_kernel,
    point_weight,
    column_index,
    column_weight,
    owner,
    observed,
    hidden_weight,
    level_weight,
    inverse_error,
):
    channels, height, breadth = state.shape
    obs, levels = observed.shape
    hid = hidden_weight.shape[2]
    lats, n = lax.axis_size("lat"), lax.axis_size("lon")
    slots = n * CAP
    fill = (-(channels + levels)) % 16
    pack = jnp.concatenate(
        [
            hidden_weight[0],
            jnp.pad(level_weight[0].T, ((0, fill), (0, 0))),
            jnp.pad(inverse_error, ((0, 15), (0, hid - levels))),
        ],
        axis=0,
    )
    taps = jnp.pad(depth_kernel.reshape(channels, 49).astype(F32), ((0, 0), (0, 79)))
    row0 = column_index[:, :1] // breadth
    col0 = column_index[:, :1] - row0 * breadth
    args = (
        state.transpose(1, 0, 2),
        pack,
        owner.reshape(1, obs),
        owner,
        row0,
        col0,
        column_weight,
        observed,
        taps,
        point_weight.T,
        point_weight,
    )
    rows = height + 6
    grid = (rows, channels, breadth)
    vm = pltpu.VMEM
    grad, departures = pl.pallas_call(
        lambda *refs: kernel(lats, n, *refs),
        out_shape=(
            jax.ShapeDtypeStruct((height, channels, breadth), BF),
            jax.ShapeDtypeStruct((obs, levels), BF),
        ),
        in_specs=[VM] * len(args),
        out_specs=(VM, VM),
        scratch_shapes=[
            vm(grid, BF),
            vm(grid, BF),
            vm(grid, BF),
            vm((2, height, 8, channels), BF),
            vm((2, rows, 8, channels), BF),
            vm((2, rows, 8, channels), BF),
            vm((n,) + pack.shape, BF),
            vm((height, obs, breadth), BF),
            vm((slots, obs), BF),
            vm((obs, slots), BF),
            vm((slots, levels), BF),
            vm((height, channels, breadth), BF),
            vm((height, channels, breadth), F32),
            vm((obs, channels), F32),
            vm((slots, channels), BF),
            vm((slots, channels), BF),
            vm((slots, levels), BF),
            pltpu.SemaphoreType.DMA((2, 8)),
            pltpu.SemaphoreType.DMA((2, 8)),
            pltpu.SemaphoreType.DMA((n,)),
            pltpu.SemaphoreType.DMA((n,)),
        ],
        compiler_params=pltpu.CompilerParams(
            vmem_limit_bytes=56 << 20, collective_id=0, has_side_effects=True
        ),
    )(*args)
    return (grad.transpose(1, 0, 2), departures)


def solution(mesh):
    in_specs = (
        P(None, "lat", "lon"),
        P(),
        P(),
        P(("lat", "lon"), None),
        P(("lat", "lon"), None),
        P(("lat", "lon"), None),
        P(("lat", "lon"), None),
        P("lon", None, None),
        P("lon", None, None),
        P("lon", None),
    )
    out_specs = (P(None, "lat", "lon"), P(("lat", "lon"), None))
    return jax.shard_map(body, mesh=mesh, in_specs=in_specs, out_specs=out_specs, check_vma=False)
```

```python
import jax
import jax.numpy as jnp
from jax import lax
from jax.experimental import pallas as pl
from jax.experimental.pallas import tpu as pltpu
from jax.sharding import PartitionSpec as P

CAP = 64
F32 = jnp.float32
BF = jnp.bfloat16
VM = pl.BlockSpec(memory_space=pltpu.VMEM)


def nn(a, b):
    return jnp.dot(a, b, preferred_element_type=F32)


def nt(a, b):
    return lax.dot_general(a, b, (((1,), (1,)), ((), ())), preferred_element_type=F32)


def conv_group(x_ref, h_ref, k_ref, base, flip):
    rows = x_ref.shape[0]
    breadth = x_ref.shape[2]
    height = rows - 6
    lane = lax.broadcasted_iota(jnp.int32, (16, breadth), 1)
    taps = k_ref[pl.ds(base, 16), :]
    total = [None] * height
    for start in range(0, 7, 2):
        part = [None] * height
        for col in range(start, min(start + 2, 7)):
            shift = col - 3
            weights = []
            for row in range(7):
                t = (6 - row) * 8 + 6 - col if flip else row * 8 + col
                weights.append(jnp.broadcast_to(taps[:, t : t + 1], (16, breadth)))
            for r in range(rows):
                v = x_ref[r, pl.ds(base, 16), :]
                if shift:
                    edge = h_ref[r, pl.ds(base, 16), :]
                    mask = lane < shift if shift > 0 else lane >= breadth + shift
                    v = pltpu.roll(jnp.where(mask, edge, v), (-shift) % breadth, 1)
                for row in range(7):
                    i = r - row
                    if 0 <= i < height:
                        term = weights[row] * v
                        part[i] = term if part[i] is None else part[i] + term
        for i in range(height):
            wide = part[i].astype(F32)
            total[i] = wide if total[i] is None else total[i] + wide
    return total


def prepare(owner, index, weight, obs_t, meta, wt_ref, p_ref, pt_ref, obs_slot):
    height, obs, breadth = wt_ref.shape
    slots = p_ref.shape[0]
    n = slots // CAP
    si = lax.broadcasted_iota(jnp.int32, (obs, obs), 0)
    sj = lax.broadcasted_iota(jnp.int32, (obs, obs), 1)
    earlier = jnp.where(si < sj, 1.0, 0.0).astype(BF)
    own = owner[...]
    hot = jnp.where(lax.broadcasted_iota(jnp.int32, (n, obs), 0) == own, 1.0, 0.0)
    within = jnp.sum(nn(hot.astype(BF), earlier) * hot, axis=0, keepdims=True)
    slot_row = own * CAP + within.astype(jnp.int32)
    corner = index[0:1, :].astype(F32)
    row0 = jnp.floor((corner + 0.5) / breadth)
    meta[...] = jnp.zeros_like(meta)
    meta[0:4, :] = weight[...].astype(F32)
    meta[4:5, :] = row0
    meta[5:6, :] = corner - row0 * breadth
    meta[6:7, :] = slot_row.astype(F32)
    by_obs = meta[...].T
    w = by_obs[:, 0:4]
    whole = by_obs.astype(jnp.int32)
    lane = lax.broadcasted_iota(jnp.int32, (obs, breadth), 1)
    r0 = jnp.broadcast_to(whole[:, 4:5], (obs, breadth))
    c0 = jnp.broadcast_to(whole[:, 5:6], (obs, breadth))
    zero = jnp.zeros((obs, breadth), F32)
    first = lane == c0
    second = lane == c0 + 1
    top = jnp.where(first, w[:, 0:1], jnp.where(second, w[:, 1:2], zero))
    bottom = jnp.where(first, w[:, 2:3], jnp.where(second, w[:, 3:4], zero))
    for r in range(height):
        wt_ref[r] = jnp.where(r0 == r, top, jnp.where(r0 == r - 1, bottom, zero)).astype(BF)
    place = lax.broadcasted_iota(jnp.int32, (slots, obs), 0) == slot_row
    p = jnp.where(place, 1.0, 0.0).astype(BF)
    p_ref[...] = p
    place = lax.broadcasted_iota(jnp.int32, (obs, slots), 1) == whole[:, 6:7]
    pt_ref[...] = jnp.where(place, 1.0, 0.0).astype(BF)
    obs_slot[...] = nt(p, obs_t[...]).astype(BF)


def remote(src, dst, send, recv, device):
    return pltpu.make_async_remote_copy(
        src_ref=src,
        dst_ref=dst,
        send_sem=send,
        recv_sem=recv,
        device_id=device,
        device_id_type=pl.DeviceIdType.MESH,
    )


def selector(breadth):
    s = lax.broadcasted_iota(jnp.int32, (8, breadth), 0)
    lane = lax.broadcasted_iota(jnp.int32, (8, breadth), 1)
    near = (s < 3) & (lane == s)
    far = (s > 4) & (lane == s + (breadth - 8))
    return jnp.where(near | far, 1.0, 0.0).astype(BF)


def copies(src, off, x, edge, right_in, left_in, send, recv, lats, lons):
    height = edge.shape[0]
    lat, lon = lax.axis_index("lat"), lax.axis_index("lon")
    left, right = lax.rem(lon + lons - 1, lons), lax.rem(lon + 1, lons)
    low, high, mid = pl.ds(0, 3), pl.ds(height + 3, 3), pl.ds(3, height)
    end = pl.ds(height - 3, 3)

    def make(i, a, b, device):
        return remote(a, b, send.at[i], recv.at[i], device)

    side = [
        make(2, edge, right_in.at[mid], {"lat": lat, "lon": left}),
        make(3, edge, left_in.at[mid], {"lat": lat, "lon": right}),
    ]
    u, d = lax.max(lat - 1, 0), lax.min(lat + 1, lats - 1)
    up = [
        make(0, src.at[pl.ds(off, 3)], x.at[high], {"lat": u, "lon": lon}),
        make(4, edge.at[low], right_in.at[high], {"lat": u, "lon": left}),
        make(5, edge.at[low], left_in.at[high], {"lat": u, "lon": right}),
    ]
    down = [
        make(1, src.at[pl.ds(off + height - 3, 3)], x.at[low], {"lat": d, "lon": lon}),
        make(6, edge.at[end], right_in.at[low], {"lat": d, "lon": left}),
        make(7, edge.at[end], left_in.at[low], {"lat": d, "lon": right}),
    ]
    return lat > 0, lat < lats - 1, up, down, side


def make_edges(src, edge):
    pick = selector(src.shape[2])

    def row(r, carry):
        edge[r] = nt(pick, src[3 + r]).astype(BF)
        return carry

    lax.fori_loop(0, edge.shape[0], row, 0, unroll=4)


def start_exchange(x, edge, right_in, left_in, send, recv, lats, lons):
    height = edge.shape[0]
    has_up, has_down, up, down, side = copies(
        x, 3, x, edge, right_in, left_in, send, recv, lats, lons
    )

    @pl.when(has_up)
    def _():
        for copy in up:
            copy.start()

    @pl.when(has_down)
    def _():
        for copy in down:
            copy.start()

    for copy in side:
        copy.start()
    for has, at in ((has_up, 0), (has_down, height + 3)):

        @pl.when(jnp.logical_not(has))
        def _():
            for ref in (x, right_in, left_in):
                ref[at : at + 3] = jnp.zeros((3,) + ref.shape[1:], BF)


def end_exchange(x, edge, right_in, left_in, halo, send, recv, lats, lons):
    has_up, has_down, up, down, side = copies(
        x, 3, x, edge, right_in, left_in, send, recv, lats, lons
    )

    @pl.when(has_up)
    def _():
        for copy in down:
            copy.wait_recv()
        for copy in up:
            copy.wait_send()

    @pl.when(has_down)
    def _():
        for copy in up:
            copy.wait_recv()
        for copy in down:
            copy.wait_send()

    for copy in side:
        copy.wait()
    pick = selector(x.shape[2])
    near = lax.broadcasted_iota(jnp.int32, (8, x.shape[1]), 0) < 4

    def row(r, carry):
        both = jnp.where(near, right_in[r].astype(F32), left_in[r].astype(F32))
        halo[r] = nn(both.T.astype(BF), pick).astype(BF)
        return carry

    lax.fori_loop(0, x.shape[0], row, 0, unroll=2)


def kernel(
    lats,
    lons,
    state,
    hw_ref,
    lw_ref,
    err_ref,
    owner,
    index,
    weight,
    obs_t,
    k_ref,
    pw_ref,
    out_ref,
    dep_ref,
    x1,
    x2,
    stage,
    meta,
    tap_rows,
    taps,
    pwt,
    halo,
    edge,
    right_in,
    left_in,
    ops,
    wt,
    p_mat,
    pt_mat,
    obs_slot,
    mixed,
    grid_f,
    total,
    prof,
    adj,
    mis,
    send,
    recv,
    op_send,
    op_recv,
):
    channels, height, breadth = state.shape
    levels = obs_t.shape[0]
    err_row = ops.shape[1] - 16
    lat, lon = lax.axis_index("lat"), lax.axis_index("lon")
    partner = lon + 1 - 2 * lax.rem(lon, 2)
    other = lax.rem(lon + lons - 1 + 2 * lax.rem(lon, 2), lons)
    half = lons // 2
    peers = [lax.rem(lon + 2 * j, lons) for j in range(1, half)]
    barrier = pltpu.get_barrier_semaphore()

    def greet(a, b):
        pl.semaphore_signal(
            barrier,
            inc=1,
            device_id={"lat": a, "lon": b},
            device_id_type=pl.DeviceIdType.MESH,
        )

    for b in [partner, other] + peers:
        greet(lat, b)

    @pl.when(lat > 0)
    def _():
        for b in (partner, lon, other):
            greet(lat - 1, b)

    @pl.when(lat < lats - 1)
    def _():
        for b in (partner, lon, other):
            greet(lat + 1, b)

    def turn(g, carry):
        at = pl.ds(pl.multiple_of(g * 16, 16), 16)
        stage[...] = state[at].astype(F32)
        for r in range(height):
            x1[3 + r, at, :] = stage[:, r, :].astype(BF)
        return carry

    lax.fori_loop(0, channels // 16, turn, 0)

    def wires(k):
        return edge.at[k], right_in.at[k], left_in.at[k]

    make_edges(x1, edge.at[0])
    ops[lon] = jnp.zeros(ops.shape[1:], BF)
    ops[lon, :channels, :] = hw_ref[0]
    ops[lon, channels : channels + levels, :] = lw_ref[0]
    ops[lon, err_row : err_row + 1, :levels] = err_ref[...]
    sides = lax.min(lat, 1) + lax.min(lats - 1 - lat, 1)
    pl.semaphore_wait(barrier, half + 1 + 3 * sides)
    start_exchange(x1, *wires(0), send.at[0], recv.at[0], lats, lons)
    mine = ops.at[lon]
    sends = [
        remote(mine, mine, op_send.at[j], op_recv.at[lon], {"lat": lat, "lon": b})
        for j, b in enumerate([partner] + peers)
    ]
    for copy in sends:
        copy.start()
    tap_rows[...] = jnp.zeros_like(tap_rows)
    for row in range(7):
        tap_rows[8 * row : 8 * row + 7, :] = k_ref[row].astype(F32)
    taps[...] = tap_rows[...].T.astype(BF)
    pwt[...] = pw_ref[...].astype(F32).T.astype(BF)
    prepare(owner, index, weight, obs_t, meta, wt, p_mat, pt_mat, obs_slot)
    end_exchange(x1, *wires(0), halo, send.at[0], recv.at[0], lats, lons)

    def group(g, carry):
        base = pl.multiple_of(g * 16, 16)
        for i, v in enumerate(conv_group(x1, halo, taps, base, False)):
            mixed[i, pl.ds(base, 16), :] = v.astype(BF)
        return carry

    lax.fori_loop(0, channels // 16, group, 0)

    forwards = []
    for j, b in enumerate(peers):
        copy = remote(
            ops.at[b], ops.at[b], op_send.at[half + j], op_recv.at[b], {"lat": lat, "lon": partner}
        )
        copy.wait_recv()
        copy.start()
        forwards.append(copy)

    total[...] = jnp.zeros_like(total)
    a, c3 = 0.7978845608028654, 0.044715

    def ahead(q, carry):
        r = q * 2
        pre = nn(pwt[...], jnp.concatenate([mixed[r], mixed[r + 1]], axis=1))
        square = pre * pre
        t = jnp.tanh(a * (pre + c3 * (square * pre)))
        gate = 0.5 * (1.0 + t)
        slope = gate + (0.5 * pre) * (1.0 - t * t) * (a * (1.0 + (3.0 * c3) * square))
        grid_f[r] = slope[:, :breadth]
        grid_f[r + 1] = slope[:, breadth:]
        here = jnp.concatenate([x1[r + 3], x1[r + 4]], axis=1).astype(F32)
        analysis = (here + pre * gate).astype(BF)
        total[...] += nt(jnp.concatenate([wt[r], wt[r + 1]], axis=1), analysis)
        return carry

    lax.fori_loop(0, height // 2, ahead, 0)
    prof[...] = nn(p_mat[...], total[...].astype(BF)).astype(BF)

    for j in range(half):
        b = lax.rem(partner + 2 * j, lons)
        remote(
            ops.at[b], ops.at[b], op_send.at[0], op_recv.at[b], {"lat": lat, "lon": partner}
        ).wait_recv()

    def instrument(o, carry):
        at = pl.ds(pl.multiple_of(o * CAP, CAP), CAP)
        hw = ops[o, :channels, :]
        lw = ops[o, channels : channels + levels, :]
        err = ops[o, err_row : err_row + 1, :levels].astype(F32)
        squashed = jnp.tanh(nn(prof[at, :], hw))
        misfit = nt(squashed.astype(BF), lw) - obs_slot[at, :].astype(F32)
        mis[at, :] = misfit.astype(BF)
        back = nn((err * misfit).astype(BF), lw) * (1.0 - squashed * squashed)
        adj[at, :] = nt(back.astype(BF), hw).astype(BF)
        return carry

    lax.fori_loop(0, lons, instrument, 0, unroll=4)
    dep_ref[...] = nn(pt_mat[...], mis[...]).T.astype(BF)
    adj_t = nn(pt_mat[...], adj[...]).T.astype(BF)

    def behind(q, carry):
        r = q * 2
        fb = nn(adj_t, jnp.concatenate([wt[r], wt[r + 1]], axis=1))
        gate = (fb * jnp.concatenate([grid_f[r], grid_f[r + 1]], axis=1)).astype(BF)
        grid_f[r] = fb[:, :breadth]
        grid_f[r + 1] = fb[:, breadth:]
        mb = nn(pw_ref[...], gate).astype(BF)
        x2[r + 3] = mb[:, :breadth]
        x2[r + 4] = mb[:, breadth:]
        return carry

    lax.fori_loop(0, height // 2, behind, 0)
    for copy in sends + forwards:
        copy.wait_send()
    make_edges(x2, edge.at[1])
    start_exchange(x2, *wires(1), send.at[1], recv.at[1], lats, lons)
    end_exchange(x2, *wires(1), halo, send.at[1], recv.at[1], lats, lons)

    def group_back(g, carry):
        base = pl.multiple_of(g * 16, 16)
        for i, v in enumerate(conv_group(x2, halo, taps, base, True)):
            stage[:, i, :] = v + grid_f[i, pl.ds(base, 16), :]
        out_ref[pl.ds(base, 16)] = stage[...].astype(BF)
        return carry

    lax.fori_loop(0, channels // 16, group_back, 0)


def body(
    state,
    depth_kernel,
    point_weight,
    column_index,
    column_weight,
    owner,
    observed,
    hidden_weight,
    level_weight,
    inverse_error,
):
    channels, height, breadth = state.shape
    obs, levels = observed.shape
    hid = hidden_weight.shape[2]
    lats, n = lax.axis_size("lat"), lax.axis_size("lon")
    slots = n * CAP
    depth = channels + levels + (-(channels + levels)) % 16 + 16
    args = (
        state,
        hidden_weight,
        level_weight.transpose(0, 2, 1),
        inverse_error,
        owner.T,
        column_index.T,
        column_weight.T,
        observed.T,
        depth_kernel.transpose(1, 2, 0),
        point_weight,
    )
    rows = height + 6
    grid = (rows, channels, breadth)
    vm = pltpu.VMEM
    grad, departures = pl.pallas_call(
        lambda *refs: kernel(lats, n, *refs),
        out_shape=(
            jax.ShapeDtypeStruct((channels, height, breadth), BF),
            jax.ShapeDtypeStruct((levels, obs), BF),
        ),
        in_specs=[VM] * len(args),
        out_specs=(VM, VM),
        scratch_shapes=[
            vm(grid, BF),
            vm(grid, BF),
            vm((16, height, breadth), F32),
            vm((8, obs), F32),
            vm((64, channels), F32),
            vm((channels, 64), BF),
            vm((channels, channels), BF),
            vm(grid, BF),
            vm((2, height, 8, channels), BF),
            vm((2, rows, 8, channels), BF),
            vm((2, rows, 8, channels), BF),
            vm((n, depth, hid), BF),
            vm((height, obs, breadth), BF),
            vm((slots, obs), BF),
            vm((obs, slots), BF),
            vm((slots, levels), BF),
            vm((height, channels, breadth), BF),
            vm((height, channels, breadth), F32),
            vm((obs, channels), F32),
            vm((slots, channels), BF),
            vm((slots, channels), BF),
            vm((slots, levels), BF),
            pltpu.SemaphoreType.DMA((2, 8)),
            pltpu.SemaphoreType.DMA((2, 8)),
            pltpu.SemaphoreType.DMA((n,)),
            pltpu.SemaphoreType.DMA((n,)),
        ],
        compiler_params=pltpu.CompilerParams(
            vmem_limit_bytes=56 << 20, collective_id=0, has_side_effects=True
        ),
    )(*args)
    return (grad, departures.T)


def solution(mesh):
    in_specs = (
        P(None, "lat", "lon"),
        P(),
        P(),
        P(("lat", "lon"), None),
        P(("lat", "lon"), None),
        P(("lat", "lon"), None),
        P(("lat", "lon"), None),
        P("lon", None, None),
        P("lon", None, None),
        P("lon", None),
    )
    out_specs = (P(None, "lat", "lon"), P(("lat", "lon"), None))
    return jax.shard_map(body, mesh=mesh, in_specs=in_specs, out_specs=out_specs, check_vma=False)
```

```python
import jax
import jax.numpy as jnp
from jax import lax
from jax.experimental import pallas as pl
from jax.experimental.pallas import tpu as pltpu
from jax.sharding import PartitionSpec as P

CAP = 64
F32 = jnp.float32
BF = jnp.bfloat16
VM = pl.BlockSpec(memory_space=pltpu.VMEM)


def nn(a, b):
    return jnp.dot(a, b, preferred_element_type=F32)


def nt(a, b):
    return lax.dot_general(a, b, (((1,), (1,)), ((), ())), preferred_element_type=F32)


def conv_group(x_ref, h_ref, k_ref, base, flip):
    rows = x_ref.shape[0]
    breadth = x_ref.shape[2]
    height = rows - 6
    lane = lax.broadcasted_iota(jnp.int32, (16, breadth), 1)
    taps = k_ref[pl.ds(base, 16), :]
    acc = [None] * height
    for col in range(7):
        shift = col - 3
        weights = []
        for row in range(7):
            t = (6 - row) * 8 + 6 - col if flip else row * 8 + col
            weights.append(jnp.broadcast_to(taps[:, t : t + 1], (16, breadth)))
        for r in range(rows):
            v = x_ref[r, pl.ds(base, 16), :].astype(F32)
            if shift:
                edge = h_ref[r, pl.ds(base, 16), :].astype(F32)
                mask = lane < shift if shift > 0 else lane >= breadth + shift
                v = pltpu.roll(jnp.where(mask, edge, v), (-shift) % breadth, 1)
            for row in range(7):
                i = r - row
                if 0 <= i < height:
                    term = weights[row] * v
                    acc[i] = term if acc[i] is None else acc[i] + term
    return acc


def prepare(owner, index, weight, obs_t, meta, wt_ref, p_ref, pt_ref, obs_slot):
    height, obs, breadth = wt_ref.shape
    slots = p_ref.shape[0]
    n = slots // CAP
    si = lax.broadcasted_iota(jnp.int32, (obs, obs), 0)
    sj = lax.broadcasted_iota(jnp.int32, (obs, obs), 1)
    earlier = jnp.where(si < sj, 1.0, 0.0).astype(BF)
    own = owner[...]
    hot = jnp.where(lax.broadcasted_iota(jnp.int32, (n, obs), 0) == own, 1.0, 0.0)
    within = jnp.sum(nn(hot.astype(BF), earlier) * hot, axis=0, keepdims=True)
    slot_row = own * CAP + within.astype(jnp.int32)
    corner = index[0:1, :].astype(F32)
    row0 = jnp.floor((corner + 0.5) / breadth)
    meta[...] = jnp.zeros_like(meta)
    meta[0:4, :] = weight[...].astype(F32)
    meta[4:5, :] = row0
    meta[5:6, :] = corner - row0 * breadth
    meta[6:7, :] = slot_row.astype(F32)
    by_obs = meta[...].T
    w = by_obs[:, 0:4]
    whole = by_obs.astype(jnp.int32)
    lane = lax.broadcasted_iota(jnp.int32, (obs, breadth), 1)
    r0 = jnp.broadcast_to(whole[:, 4:5], (obs, breadth))
    c0 = jnp.broadcast_to(whole[:, 5:6], (obs, breadth))
    zero = jnp.zeros((obs, breadth), F32)
    first = lane == c0
    second = lane == c0 + 1
    top = jnp.where(first, w[:, 0:1], jnp.where(second, w[:, 1:2], zero))
    bottom = jnp.where(first, w[:, 2:3], jnp.where(second, w[:, 3:4], zero))
    for r in range(height):
        wt_ref[r] = jnp.where(r0 == r, top, jnp.where(r0 == r - 1, bottom, zero)).astype(BF)
    place = lax.broadcasted_iota(jnp.int32, (slots, obs), 0) == slot_row
    p = jnp.where(place, 1.0, 0.0).astype(BF)
    p_ref[...] = p
    place = lax.broadcasted_iota(jnp.int32, (obs, slots), 1) == whole[:, 6:7]
    pt_ref[...] = jnp.where(place, 1.0, 0.0).astype(BF)
    obs_slot[...] = nt(p, obs_t[...]).astype(BF)


def remote(src, dst, send, recv, device):
    return pltpu.make_async_remote_copy(
        src_ref=src,
        dst_ref=dst,
        send_sem=send,
        recv_sem=recv,
        device_id=device,
        device_id_type=pl.DeviceIdType.MESH,
    )


def selector(breadth):
    s = lax.broadcasted_iota(jnp.int32, (8, breadth), 0)
    lane = lax.broadcasted_iota(jnp.int32, (8, breadth), 1)
    near = (s < 3) & (lane == s)
    far = (s > 4) & (lane == s + (breadth - 8))
    return jnp.where(near | far, 1.0, 0.0).astype(BF)


def copies(src, off, x, edge, right_in, left_in, send, recv, lats, lons):
    height = edge.shape[0]
    lat, lon = lax.axis_index("lat"), lax.axis_index("lon")
    left, right = lax.rem(lon + lons - 1, lons), lax.rem(lon + 1, lons)
    low, high, mid = pl.ds(0, 3), pl.ds(height + 3, 3), pl.ds(3, height)
    end = pl.ds(height - 3, 3)

    def make(i, a, b, device):
        return remote(a, b, send.at[i], recv.at[i], device)

    side = [
        make(2, edge, right_in.at[mid], {"lat": lat, "lon": left}),
        make(3, edge, left_in.at[mid], {"lat": lat, "lon": right}),
    ]
    u, d = lax.max(lat - 1, 0), lax.min(lat + 1, lats - 1)
    up = [
        make(0, src.at[pl.ds(off, 3)], x.at[high], {"lat": u, "lon": lon}),
        make(4, edge.at[low], right_in.at[high], {"lat": u, "lon": left}),
        make(5, edge.at[low], left_in.at[high], {"lat": u, "lon": right}),
    ]
    down = [
        make(1, src.at[pl.ds(off + height - 3, 3)], x.at[low], {"lat": d, "lon": lon}),
        make(6, edge.at[end], right_in.at[low], {"lat": d, "lon": left}),
        make(7, edge.at[end], left_in.at[low], {"lat": d, "lon": right}),
    ]
    return lat > 0, lat < lats - 1, up, down, side


def make_edges(src, edge):
    pick = selector(src.shape[2])

    def row(r, carry):
        edge[r] = nt(pick, src[3 + r]).astype(BF)
        return carry

    lax.fori_loop(0, edge.shape[0], row, 0, unroll=4)


def start_exchange(x, edge, right_in, left_in, send, recv, lats, lons):
    height = edge.shape[0]
    has_up, has_down, up, down, side = copies(
        x, 3, x, edge, right_in, left_in, send, recv, lats, lons
    )

    @pl.when(has_up)
    def _():
        for copy in up:
            copy.start()

    @pl.when(has_down)
    def _():
        for copy in down:
            copy.start()

    for copy in side:
        copy.start()
    for has, at in ((has_up, 0), (has_down, height + 3)):

        @pl.when(jnp.logical_not(has))
        def _():
            for ref in (x, right_in, left_in):
                ref[at : at + 3] = jnp.zeros((3,) + ref.shape[1:], BF)


def end_exchange(x, edge, right_in, left_in, halo, send, recv, lats, lons):
    has_up, has_down, up, down, side = copies(
        x, 3, x, edge, right_in, left_in, send, recv, lats, lons
    )

    @pl.when(has_up)
    def _():
        for copy in down:
            copy.wait_recv()
        for copy in up:
            copy.wait_send()

    @pl.when(has_down)
    def _():
        for copy in up:
            copy.wait_recv()
        for copy in down:
            copy.wait_send()

    for copy in side:
        copy.wait()
    pick = selector(x.shape[2])
    near = lax.broadcasted_iota(jnp.int32, (8, x.shape[1]), 0) < 4

    def row(r, carry):
        both = jnp.where(near, right_in[r].astype(F32), left_in[r].astype(F32))
        halo[r] = nn(both.T.astype(BF), pick).astype(BF)
        return carry

    lax.fori_loop(0, x.shape[0], row, 0, unroll=2)


def kernel(
    lats,
    lons,
    state,
    hw_ref,
    lw_ref,
    err_ref,
    owner,
    index,
    weight,
    obs_t,
    k_ref,
    pw_ref,
    out_ref,
    dep_ref,
    x1,
    x2,
    stage,
    meta,
    tap_rows,
    taps,
    pwt,
    halo,
    edge,
    right_in,
    left_in,
    ops,
    wt,
    p_mat,
    pt_mat,
    obs_slot,
    mixed,
    grid_f,
    total,
    prof,
    adj,
    mis,
    send,
    recv,
    op_send,
    op_recv,
):
    channels, height, breadth = state.shape
    levels = obs_t.shape[0]
    err_row = ops.shape[1] - 16
    lat, lon = lax.axis_index("lat"), lax.axis_index("lon")
    partner = lon + 1 - 2 * lax.rem(lon, 2)
    other = lax.rem(lon + lons - 1 + 2 * lax.rem(lon, 2), lons)
    half = lons // 2
    peers = [lax.rem(lon + 2 * j, lons) for j in range(1, half)]
    barrier = pltpu.get_barrier_semaphore()

    def greet(a, b):
        pl.semaphore_signal(
            barrier,
            inc=1,
            device_id={"lat": a, "lon": b},
            device_id_type=pl.DeviceIdType.MESH,
        )

    for b in [partner, other] + peers:
        greet(lat, b)

    @pl.when(lat > 0)
    def _():
        for b in (partner, lon, other):
            greet(lat - 1, b)

    @pl.when(lat < lats - 1)
    def _():
        for b in (partner, lon, other):
            greet(lat + 1, b)

    def turn(g, carry):
        at = pl.ds(pl.multiple_of(g * 16, 16), 16)
        stage[...] = state[at].astype(F32)
        for r in range(height):
            x1[3 + r, at, :] = stage[:, r, :].astype(BF)
        return carry

    lax.fori_loop(0, channels // 16, turn, 0)

    def wires(k):
        return edge.at[k], right_in.at[k], left_in.at[k]

    make_edges(x1, edge.at[0])
    ops[lon] = jnp.zeros(ops.shape[1:], BF)
    ops[lon, :channels, :] = hw_ref[0]
    ops[lon, channels : channels + levels, :] = lw_ref[0]
    ops[lon, err_row : err_row + 1, :levels] = err_ref[...]
    sides = lax.min(lat, 1) + lax.min(lats - 1 - lat, 1)
    pl.semaphore_wait(barrier, half + 1 + 3 * sides)
    start_exchange(x1, *wires(0), send.at[0], recv.at[0], lats, lons)
    mine = ops.at[lon]
    sends = [
        remote(mine, mine, op_send.at[j], op_recv.at[lon], {"lat": lat, "lon": b})
        for j, b in enumerate([partner] + peers)
    ]
    for copy in sends:
        copy.start()
    tap_rows[...] = jnp.zeros_like(tap_rows)
    for row in range(7):
        tap_rows[8 * row : 8 * row + 7, :] = k_ref[row].astype(F32)
    taps[...] = tap_rows[...].T
    pwt[...] = pw_ref[...].astype(F32).T.astype(BF)
    prepare(owner, index, weight, obs_t, meta, wt, p_mat, pt_mat, obs_slot)
    end_exchange(x1, *wires(0), halo, send.at[0], recv.at[0], lats, lons)

    def group(g, carry):
        base = pl.multiple_of(g * 16, 16)
        for i, v in enumerate(conv_group(x1, halo, taps, base, False)):
            mixed[i, pl.ds(base, 16), :] = v.astype(BF)
        return carry

    lax.fori_loop(0, channels // 16, group, 0)

    forwards = []
    for j, b in enumerate(peers):
        copy = remote(
            ops.at[b], ops.at[b], op_send.at[half + j], op_recv.at[b], {"lat": lat, "lon": partner}
        )
        copy.wait_recv()
        copy.start()
        forwards.append(copy)

    total[...] = jnp.zeros_like(total)
    a, c3 = 0.7978845608028654, 0.044715

    def ahead(q, carry):
        r = q * 2
        pre = nn(pwt[...], jnp.concatenate([mixed[r], mixed[r + 1]], axis=1))
        square = pre * pre
        t = jnp.tanh(a * (pre + c3 * (square * pre)))
        gate = 0.5 * (1.0 + t)
        slope = gate + (0.5 * pre) * (1.0 - t * t) * (a * (1.0 + (3.0 * c3) * square))
        grid_f[r] = slope[:, :breadth]
        grid_f[r + 1] = slope[:, breadth:]
        here = jnp.concatenate([x1[r + 3], x1[r + 4]], axis=1).astype(F32)
        analysis = (here + pre * gate).astype(BF)
        total[...] += nt(jnp.concatenate([wt[r], wt[r + 1]], axis=1), analysis)
        return carry

    lax.fori_loop(0, height // 2, ahead, 0)
    prof[...] = nn(p_mat[...], total[...].astype(BF)).astype(BF)

    for j in range(half):
        b = lax.rem(partner + 2 * j, lons)
        remote(
            ops.at[b], ops.at[b], op_send.at[0], op_recv.at[b], {"lat": lat, "lon": partner}
        ).wait_recv()

    def instrument(o, carry):
        at = pl.ds(pl.multiple_of(o * CAP, CAP), CAP)
        hw = ops[o, :channels, :]
        lw = ops[o, channels : channels + levels, :]
        err = ops[o, err_row : err_row + 1, :levels].astype(F32)
        squashed = jnp.tanh(nn(prof[at, :], hw))
        misfit = nt(squashed.astype(BF), lw) - obs_slot[at, :].astype(F32)
        mis[at, :] = misfit.astype(BF)
        back = nn((err * misfit).astype(BF), lw) * (1.0 - squashed * squashed)
        adj[at, :] = nt(back.astype(BF), hw).astype(BF)
        return carry

    lax.fori_loop(0, lons, instrument, 0, unroll=4)
    dep_ref[...] = nn(pt_mat[...], mis[...]).T.astype(BF)
    adj_t = nn(pt_mat[...], adj[...]).T.astype(BF)

    def behind(q, carry):
        r = q * 2
        fb = nn(adj_t, jnp.concatenate([wt[r], wt[r + 1]], axis=1))
        gate = (fb * jnp.concatenate([grid_f[r], grid_f[r + 1]], axis=1)).astype(BF)
        grid_f[r] = fb[:, :breadth]
        grid_f[r + 1] = fb[:, breadth:]
        mb = nn(pw_ref[...], gate).astype(BF)
        x2[r + 3] = mb[:, :breadth]
        x2[r + 4] = mb[:, breadth:]
        return carry

    lax.fori_loop(0, height // 2, behind, 0)
    for copy in sends + forwards:
        copy.wait_send()
    make_edges(x2, edge.at[1])
    start_exchange(x2, *wires(1), send.at[1], recv.at[1], lats, lons)
    end_exchange(x2, *wires(1), halo, send.at[1], recv.at[1], lats, lons)

    def group_back(g, carry):
        base = pl.multiple_of(g * 16, 16)
        for i, v in enumerate(conv_group(x2, halo, taps, base, True)):
            stage[:, i, :] = v + grid_f[i, pl.ds(base, 16), :]
        out_ref[pl.ds(base, 16)] = stage[...].astype(BF)
        return carry

    lax.fori_loop(0, channels // 16, group_back, 0)


def body(
    state,
    depth_kernel,
    point_weight,
    column_index,
    column_weight,
    owner,
    observed,
    hidden_weight,
    level_weight,
    inverse_error,
):
    channels, height, breadth = state.shape
    obs, levels = observed.shape
    hid = hidden_weight.shape[2]
    lats, n = lax.axis_size("lat"), lax.axis_size("lon")
    slots = n * CAP
    depth = channels + levels + (-(channels + levels)) % 16 + 16
    args = (
        state,
        hidden_weight,
        level_weight.transpose(0, 2, 1),
        inverse_error,
        owner.T,
        column_index.T,
        column_weight.T,
        observed.T,
        depth_kernel.transpose(1, 2, 0),
        point_weight,
    )
    rows = height + 6
    grid = (rows, channels, breadth)
    vm = pltpu.VMEM
    grad, departures = pl.pallas_call(
        lambda *refs: kernel(lats, n, *refs),
        out_shape=(
            jax.ShapeDtypeStruct((channels, height, breadth), BF),
            jax.ShapeDtypeStruct((levels, obs), BF),
        ),
        in_specs=[VM] * len(args),
        out_specs=(VM, VM),
        scratch_shapes=[
            vm(grid, BF),
            vm(grid, BF),
            vm((16, height, breadth), F32),
            vm((8, obs), F32),
            vm((64, channels), F32),
            vm((channels, 64), F32),
            vm((channels, channels), BF),
            vm(grid, BF),
            vm((2, height, 8, channels), BF),
            vm((2, rows, 8, channels), BF),
            vm((2, rows, 8, channels), BF),
            vm((n, depth, hid), BF),
            vm((height, obs, breadth), BF),
            vm((slots, obs), BF),
            vm((obs, slots), BF),
            vm((slots, levels), BF),
            vm((height, channels, breadth), BF),
            vm((height, channels, breadth), F32),
            vm((obs, channels), F32),
            vm((slots, channels), BF),
            vm((slots, channels), BF),
            vm((slots, levels), BF),
            pltpu.SemaphoreType.DMA((2, 8)),
            pltpu.SemaphoreType.DMA((2, 8)),
            pltpu.SemaphoreType.DMA((n,)),
            pltpu.SemaphoreType.DMA((n,)),
        ],
        compiler_params=pltpu.CompilerParams(
            vmem_limit_bytes=56 << 20, collective_id=0, has_side_effects=True
        ),
    )(*args)
    return (grad, departures.T)


def solution(mesh):
    in_specs = (
        P(None, "lat", "lon"),
        P(),
        P(),
        P(("lat", "lon"), None),
        P(("lat", "lon"), None),
        P(("lat", "lon"), None),
        P(("lat", "lon"), None),
        P("lon", None, None),
        P("lon", None, None),
        P("lon", None),
    )
    out_specs = (P(None, "lat", "lon"), P(("lat", "lon"), None))
    return jax.shard_map(body, mesh=mesh, in_specs=in_specs, out_specs=out_specs, check_vma=False)
```
